32 devices in a mesh: tm: 8 (over y, x, core), obj: 4 (over z).
Axes of the slice: x: 2, y: 2, z: 4, core: 2. Of those that a mesh axis runs over, the one named last changes fastest.
Arguments:
- objective: float32 [32, 768, 768], P('tm', 'obj'), parts along dimension 1, may hold values from -6 to 6
- jacobians: bfloat16 [32, 768, 768], P('tm'), may hold values from -0.21875 to 0.21875
- precond_blocks: bfloat16 [2, 32, 768, 768], P(None, 'tm'), as said below
Outputs:
- adjoint: float32 [32, 768, 768], P('tm', 'obj'), parts along dimension 1
- residual: float32 [32, 768, 768], P('tm', 'obj'), parts along dimension 1
The draws below stay inside these ranges and needn't reach their ends.
There are 4 independent parts, one for each index of `obj`. The reference program is written for one: setup_inputs(seed, part) draws one part's arguments, and reference() takes and returns one part's arrays. A program takes and returns all parts, laid end to end along the dimension named above; an argument that names none is the same for every part. Nothing has to cross between parts.
Inputs may be any that keep to these rules, and one draw needn't show every extreme that they name: precond_blocks[0, j] equals precond_blocks[0, (32 - j) mod 32] and precond_blocks[1, j] equals - precond_blocks[1, (32 - j) mod 32].
All inputs are finite; a program needn't handle non-finite values.
Results may differ from the reference program's by a relative error of at most 0.0087.
Values may be sent and summed in bfloat16 or wider, within the bound.
A program may use at most 128 MiB of HBM per device.

```python
import math
import jax
import jax.numpy as jnp
from jax import lax

NS = 768
COLS = 192
ITERS = 2
STEPS = 32


def draw_precond_blocks(key, part):
    first_key, second_key = jax.random.split(jax.random.fold_in(key, 17))
    block_shape = (STEPS, NS, NS)
    real_noise = jax.random.normal(first_key, block_shape, jnp.float32)
    imag_noise = jax.random.normal(second_key, block_shape, jnp.float32)
    mirror = (STEPS - jnp.arange(STEPS)) % STEPS
    spread = 0.8 / math.sqrt(NS)
    real_part = 0.5 * (real_noise + real_noise[mirror]) * spread + jnp.eye(NS, dtype=jnp.float32)[None]
    imag_part = 0.5 * (imag_noise - imag_noise[mirror]) * spread
    return jnp.stack([real_part, imag_part]).astype(jnp.bfloat16)


def shard_levels(rng, shape, cuts, least, top_value):
    level, own = 1.0, jax.random.fold_in(rng, 6)
    for position, shards_of in cuts:
        heights = jnp.exp(jax.random.uniform(jax.random.fold_in(own, position), (shards_of,), jnp.float32, least / len(cuts), top_value / len(cuts)))
        level = level * jnp.repeat(heights, shape[position] // shards_of).reshape([-1 if axis == position else 1 for axis in range(len(shape))])
    return level


def centred(own_key, extent, scale, reach, cuts=(), kind=jnp.bfloat16):
    array = scale * jax.random.normal(own_key, extent, jnp.float32)
    if cuts:
        array = array * shard_levels(own_key, extent, cuts, -0.22, 0.18)
    return jnp.clip(array, -reach, reach).astype(kind)


def setup_inputs(seed: int = 0, part: int = 0) -> dict:
    key_of = jax.random.split(jax.random.key(seed), 4)
    part_keys = jax.random.split(jax.random.fold_in(key_of[3], part), 4)
    return {
        "objective": centred(part_keys[0], (STEPS, COLS, NS), 1.0, 6.0, ((0, 8),), jnp.float32),
        "jacobians": centred(key_of[1], (STEPS, NS, NS), NS ** -0.5, 0.21875, ((0, 8),)),
        "precond_blocks": draw_precond_blocks(jax.random.fold_in(key_of[3], 71), part),
    }


log_alpha = math.log(0.05)


def tables(count):
    indices = jnp.arange(count, dtype=jnp.int32)
    product = (indices[:, None] * indices[None, :]) % count
    angles = product.astype(jnp.float32) * (2.0 * math.pi / count)
    return jnp.cos(angles), jnp.sin(angles)


def frequency_product(operands):
    spectrum_real, spectrum_imag, block_real, block_imag = operands
    zeta_real = spectrum_real.astype(jnp.float32)
    zeta_imag = spectrum_imag.astype(jnp.float32)
    matrix_real = block_real.astype(jnp.float32)
    matrix_imag = block_imag.astype(jnp.float32)
    highest = lax.Precision.HIGHEST
    wave_real = jnp.dot(zeta_real, matrix_real, precision=highest) - jnp.dot(zeta_imag, matrix_imag, precision=highest)
    wave_imag = jnp.dot(zeta_real, matrix_imag, precision=highest) + jnp.dot(zeta_imag, matrix_real, precision=highest)
    return wave_real.astype(jnp.bfloat16), wave_imag.astype(jnp.bfloat16)


def precondition(residual, precond_blocks):
    highest = lax.Precision.HIGHEST
    positions = jnp.arange(STEPS, dtype=jnp.float32)
    forward_scale = jnp.exp(positions * (-log_alpha / STEPS))
    inverse_factor = jnp.exp(positions * (log_alpha / STEPS)) / STEPS
    cosine_table, sine_table = tables(STEPS)
    scaled = residual * forward_scale[:, None, None]
    flattened = scaled.reshape(STEPS, -1)
    spectrum_real = jnp.dot(cosine_table, flattened, precision=highest).astype(jnp.bfloat16)
    spectrum_imag = (-jnp.dot(sine_table, flattened, precision=highest)).astype(jnp.bfloat16)
    spectrum_real = spectrum_real.reshape(STEPS, COLS, NS)
    spectrum_imag = spectrum_imag.reshape(STEPS, COLS, NS)
    wave_real, wave_imag = lax.map(frequency_product, (spectrum_real, spectrum_imag, precond_blocks[0], precond_blocks[1]))
    real_flat = wave_real.astype(jnp.float32).reshape(STEPS, -1)
    imag_flat = wave_imag.astype(jnp.float32).reshape(STEPS, -1)
    values = (jnp.dot(cosine_table, real_flat, precision=highest) - jnp.dot(sine_table, imag_flat, precision=highest)) * inverse_factor[:, None]
    return values.reshape(STEPS, COLS, NS)


def apply_operator(correction, jacobians):
    following = jnp.concatenate([correction[1:], jnp.zeros_like(correction[:1])], axis=0).astype(jnp.bfloat16)
    carried = jnp.einsum("kcn,knm->kcm", following.astype(jnp.float32), jacobians.astype(jnp.float32), precision=lax.Precision.HIGHEST)
    return correction - carried


def reference(objective, jacobians, precond_blocks):
    adjoint = jnp.zeros_like(objective)
    residual = objective
    for iteration in range(ITERS):
        correction = precondition(residual, precond_blocks)
        adjoint = adjoint + correction
        residual = residual - apply_operator(correction, jacobians)
    return adjoint, residual
```

```python
import functools
import math

import jax
import jax.numpy as jnp
import numpy as np
from jax import lax
from jax.experimental import pallas as pl
from jax.experimental.pallas import tpu as pltpu
from jax.sharding import PartitionSpec as P

ITERS = 2

log_alpha = math.log(0.05)


def make_tables(groups, local_steps):
    steps = groups * local_steps
    mid = local_steps // 2
    per_device = 4 * mid
    forward = np.zeros((groups, per_device, steps, 2))
    backward = np.zeros((steps, 2, groups, per_device))
    k = np.arange(steps)
    grow = np.exp(k * (-log_alpha / steps))
    shrink = np.exp(k * (log_alpha / steps)) / steps

    def put(t, slot, half, frequency, kind, weight):
        angle = 2.0 * math.pi * ((frequency * k) % steps) / steps
        wave = np.cos(angle) if kind == 0 else -np.sin(angle)
        forward[t, slot, :, half] = wave * grow
        backward[:, half, t, slot] = weight * wave * shrink

    for t in range(groups):
        own = 0 if t < groups // 2 else 1
        slot = 0
        for m in range(1, mid):
            for kind in range(2):
                for half in range(2):
                    put(t, slot, half, t * local_steps + m, kind, 2.0)
                    slot += 1
        for kind in range(2):
            put(t, slot, own, t * local_steps + mid, kind, 2.0)
            slot += 1
        if (2 * t) % groups == 0:
            put(t, slot, 1 - own, t * local_steps, 0, 1.0)
            put(t, slot + 1, own, t * local_steps, 0, 1.0)
        else:
            for kind in range(2):
                put(t, slot + kind, 1 - own, t * local_steps, kind, 2.0)
    return (
        forward.reshape(groups * per_device, 2 * steps),
        backward.reshape(2 * steps, groups * per_device),
    )


def split_table(table):
    high = table.astype(jnp.bfloat16)
    low = (table - high.astype(np.float64)).astype(jnp.bfloat16)
    return jnp.asarray(high), jnp.asarray(low)


def transform(table, x):
    dims = (((1,), (0,)), ((), ()))
    high, low = table
    return lax.dot_general(high, x, dims, preferred_element_type=jnp.float32) + lax.dot_general(
        low, x, dims, preferred_element_type=jnp.float32
    )


def exchange(x):
    return lax.all_to_all(x, "tm", split_axis=0, concat_axis=0, tiled=True)


def mul(left, right):
    return jnp.dot(left, right, preferred_element_type=jnp.float32)


def complex_mul(real, imag, block_real, block_imag):
    wave_real = mul(real, block_real) - mul(imag, block_imag)
    wave_imag = mul(real, block_imag) + mul(imag, block_real)
    return wave_real.astype(jnp.bfloat16), wave_imag.astype(jnp.bfloat16)


def plain_body(objective, jacobians, precond_blocks):
    local_steps, cols, ns = objective.shape
    groups = lax.axis_size("tm")
    mid = local_steps // 2
    per_device = 4 * mid
    lane_parts = 2
    row_parts = groups // lane_parts
    rows, lanes = cols // 2 // row_parts, ns // lane_parts
    forward, backward = make_tables(groups, local_steps)
    forward, backward = split_table(forward), split_table(backward)

    def to_pieces(x):
        x = x.reshape(x.shape[0], row_parts, rows, lane_parts, lanes)
        return x.transpose(1, 3, 0, 2, 4).reshape(-1, rows, lanes)

    def from_pieces(x):
        x = x.reshape(row_parts, lane_parts, -1, rows, lanes)
        return x.transpose(2, 0, 3, 1, 4).reshape(-1, cols // 2, ns)

    adjoint = jnp.zeros_like(objective)
    residual = objective
    for iteration in range(ITERS):
        sent = residual.astype(jnp.bfloat16).reshape(2 * local_steps, cols // 2, ns)
        timeline = exchange(to_pieces(sent))
        spectrum = transform(forward, timeline).astype(jnp.bfloat16)
        spectrum = from_pieces(exchange(spectrum))
        waves = []
        slot = 0
        for m in range(1, mid):
            part = spectrum[slot : slot + 4].reshape(2, cols, ns)
            pair = complex_mul(part[0], part[1], precond_blocks[0, m], precond_blocks[1, m])
            waves += [w.reshape(2, cols // 2, ns) for w in pair]
            slot += 4
        for m in (mid, 0):
            pair = complex_mul(
                spectrum[slot], spectrum[slot + 1], precond_blocks[0, m], precond_blocks[1, m]
            )
            waves += [w[None] for w in pair]
            slot += 2
        waves = exchange(to_pieces(jnp.concatenate(waves, axis=0)))
        values = transform(backward, waves).astype(jnp.bfloat16)
        correction = from_pieces(exchange(values)).reshape(local_steps, cols, ns)
        route = [(i, i - 1) for i in range(1, groups)]
        next_row = lax.ppermute(correction[:1], "tm", route)
        following = jnp.concatenate([correction[1:], next_row], axis=0)
        carried = jnp.einsum(
            "kcn,knm->kcm", following, jacobians, preferred_element_type=jnp.float32
        )
        adjoint = adjoint + correction.astype(jnp.float32)
        residual = residual - (correction.astype(jnp.float32) - carried)
    return (adjoint, residual)


def twiddle(value, angle):
    real, imag = value
    c, s = math.cos(angle), math.sin(angle)
    if imag is None:
        return real * c, real * s
    if abs(c) < 1e-12:
        return (-imag, real) if s > 0 else (imag, -real)
    if abs(s) < 1e-12:
        return value
    return real * c - imag * s, real * s + imag * c


def forward_fft(x):
    n = len(x)
    if n == 1:
        return [(x[0], None)]
    if n == 2:
        return [(x[0] + x[1], None), (x[0] - x[1], None)]
    even, odd = forward_fft(x[0::2]), forward_fft(x[1::2])
    out = [None] * (n // 2 + 1)
    out[0] = (even[0][0] + odd[0][0], None)
    out[n // 2] = (even[0][0] - odd[0][0], None)
    for k in range(1, n // 4):
        er, ei = even[k]
        tr, ti = twiddle(odd[k], -2.0 * math.pi * k / n)
        out[k] = (er + tr, ei + ti)
        out[n // 2 - k] = (er - tr, ti - ei)
    out[n // 4] = (even[n // 4][0], -odd[n // 4][0])
    return out


def backward_fft(spectrum):
    n = 2 * (len(spectrum) - 1)
    if n == 2:
        a, b = spectrum[0][0], spectrum[1][0]
        return [a + b, a - b]
    even, odd = [], []
    for k in range(n // 4 + 1):
        if k == 0:
            a, b = spectrum[0][0], spectrum[n // 2][0]
            even.append((a + b, None))
            odd.append((a - b, None))
        elif k == n // 4:
            a, b = spectrum[k]
            even.append((a + a, None))
            odd.append((-(b + b), None))
        else:
            ar, ai = spectrum[k]
            br, bi = spectrum[n // 2 - k]
            even.append((ar + br, ai - bi))
            odd.append(twiddle((ar - br, ai + bi), 2.0 * math.pi * k / n))
    out = [None] * n
    out[0::2], out[1::2] = backward_fft(even), backward_fft(odd)
    return out


def odd_position(j, steps, x):
    local_steps = steps // 8
    for held in (j, steps - j):
        t, m = held // local_steps, held % local_steps
        if (t // 2) % 2 == x:
            return ((t // 4) * 2 + t % 2) * (local_steps // 2) + m // 2
    raise ValueError(j)


def kernel(
    groups,
    parts,
    objective_hbm,
    jac_hbm,
    pre_hbm,
    adjoint_hbm,
    residual_hbm,
    adjoint,
    residual,
    weights,
    jac,
    sent,
    timeline,
    spec_even,
    spec_odd,
    in_even,
    in_odd,
    wave_even,
    wave_odd,
    back_even,
    back_odd,
    val_out,
    corr,
    lhs,
    load_sem,
    objective_sem,
    ends_send,
    ends_recv,
    own_sem,
    send_sem,
    recv_sem,
    next_own,
    next_send,
    next_recv,
    hand_send,
    hand_recv,
    out_sem,
):
    local_steps, _, ns = adjoint.shape
    steps = groups * local_steps
    pairs = local_steps // 2
    chunks, _, row_parts, _, rows, _ = sent.shape
    lanes = timeline.shape[4]
    share = row_parts * rows
    me = lax.axis_index("tm")
    part = lax.axis_index("obj")
    y, x, core = me // 4, lax.rem(me // 2, 2), lax.rem(me, 2)
    ends = (x == 0) & (core == 0)
    sign = (1 - 2 * y).astype(jnp.float32)
    f32, bf16 = jnp.float32, jnp.bfloat16

    def at_mask(mask):
        bits = [1 - v if mask & w else v for v, w in ((y, 4), (x, 2), (core, 1))]
        return bits[0] * 4 + bits[1] * 2 + bits[2]

    def row_at(a, half, c):
        return pl.ds(((a * chunks + c) * 2 + half) * rows, rows)

    def rows_of(a, c):
        return pl.ds((a * chunks + c) * 2 * rows, 2 * rows)

    fetches = [
        [
            pltpu.make_async_copy(
                objective_hbm.at[:, rows_of(a, c)],
                residual.at[:, rows_of(a, c)],
                objective_sem.at[c, a],
            )
            for a in range(row_parts)
        ]
        for c in range(chunks)
    ]
    for group in fetches:
        for fetch in group:
            fetch.start()

    load_real = pltpu.make_async_copy(pre_hbm.at[0], weights.at[0], load_sem.at[0])
    load_imag = pltpu.make_async_copy(
        pre_hbm.at[1, pl.ds(1, local_steps - 1)],
        weights.at[1, pl.ds(1, local_steps - 1)],
        load_sem.at[1],
    )
    load_first = pltpu.make_async_copy(pre_hbm.at[1, 0], weights.at[1, 0], load_sem.at[2])
    load_jac = pltpu.make_async_copy(jac_hbm, jac, load_sem.at[3])

    barrier = pltpu.get_barrier_semaphore()
    for mask in range(1, groups):
        pl.semaphore_signal(
            barrier,
            inc=1,
            device_id={"tm": at_mask(mask)},
            device_id_type=pl.DeviceIdType.MESH,
        )

    @pl.when(ends)
    def _():
        for d in range(1, parts):
            pl.semaphore_signal(
                barrier,
                inc=1,
                device_id={"obj": lax.rem(part + d, parts)},
                device_id_type=pl.DeviceIdType.MESH,
            )

    load_real.start()
    load_imag.start()
    pl.when(jnp.logical_not(ends))(load_first.start)
    load_jac.start()

    slice_rows = ns // parts
    own_slice = pl.ds(pl.multiple_of(part * slice_rows, slice_rows), slice_rows)

    def end_copy(d):
        if d == 0:
            source, target = pre_hbm.at[0, 0, own_slice], {"tm": at_mask(4)}
        else:
            source, target = weights.at[1, 0, own_slice], {"obj": lax.rem(part + d, parts)}
        return pltpu.make_async_remote_copy(
            src_ref=source,
            dst_ref=weights.at[1, 0, own_slice],
            send_sem=ends_send.at[d],
            recv_sem=ends_recv.at[d],
            device_id=target,
            device_id_type=pl.DeviceIdType.MESH,
        )

    def end_arrival(d):
        source = lax.rem(part + parts - d, parts)
        here = weights.at[1, 0, pl.ds(pl.multiple_of(source * slice_rows, slice_rows), slice_rows)]
        return pltpu.make_async_remote_copy(
            src_ref=here,
            dst_ref=here,
            send_sem=ends_send.at[d],
            recv_sem=ends_recv.at[d],
            device_id={"obj": lax.rem(part + d, parts)},
            device_id_type=pl.DeviceIdType.MESH,
        )

    def enter():
        @pl.when(ends)
        def _():
            pl.semaphore_wait(barrier, groups - 1 + parts - 1)
            end_copy(0).start()

        @pl.when(jnp.logical_not(ends))
        def _():
            pl.semaphore_wait(barrier, groups - 1)

    def pass_ends():
        @pl.when(ends)
        def _():
            end_copy(0).wait_recv()
            for d in range(1, parts):
                end_copy(d).start()

    def finish_ends():
        @pl.when(ends)
        def _():
            end_copy(0).wait_send()
            for d in range(1, parts):
                end_copy(d).wait_send()
                end_arrival(d).wait_recv()

        pl.when(jnp.logical_not(ends))(load_first.wait)

    def lane_at(p):
        return pl.ds(pl.multiple_of(lax.rem(p, 2) * lanes, lanes), lanes)

    def begin(phase, c, slot, masks, source, target):
        copies = []
        for mask in masks:
            peer = at_mask(mask)
            copy = pltpu.make_async_remote_copy(
                src_ref=source(peer),
                dst_ref=target(me),
                send_sem=send_sem.at[phase, c, slot + mask],
                recv_sem=recv_sem.at[phase, c, slot + mask],
                device_id={"tm": peer},
                device_id_type=pl.DeviceIdType.MESH,
            )
            copy.start()
            copies.append(copy)
        own = pltpu.make_async_copy(source(me), target(me), own_sem.at[phase, c, slot // groups])
        own.start()
        return copies + [own]

    everyone = (6, 2, 4, 3, 5, 7, 1)
    same_y, same_x = (2, 3, 1), (4, 5, 1)

    def finish(copies):
        for copy in copies:
            copy.wait()

    def even_rank(p):
        return lax.rem(p, 4)

    def odd_rank(p):
        return (p // 4) * 2 + lax.rem(p, 2)

    def of_rank(rank):
        return pl.ds(rank * pairs, pairs)

    def place_even(e):
        return jnp.where(y == 0, e, (steps // 4 - e) % (steps // 4))

    def place_odd(j):
        return jnp.where(x == 0, odd_position(j, steps, 0), odd_position(j, steps, 1))

    def matmul_pair(c, i, m, source, target):
        size = 4 * rows
        for kind in range(2):
            piece = source[c, i, kind].astype(f32).reshape(size, ns).astype(bf16)
            lhs[pl.ds(kind * size, size)] = piece

        @pl.loop(0, ns // 256)
        def _(n):
            at = pl.ds(pl.multiple_of(n * 256, 256), 256)
            left = lhs[pl.ds(0, 2 * size)]
            p = jnp.dot(left, weights[0, m, :, at], preferred_element_type=f32)
            q = jnp.dot(left, weights[1, m, :, at], preferred_element_type=f32)
            real = p[:size] - sign * q[size:]
            imag = sign * q[:size] + p[size:]
            if m == 0:
                real = jnp.where(ends, p[:size], real)
                imag = jnp.where(ends, q[size:], imag)
            for kind, value in enumerate((real, imag)):
                target[c, i, kind, :, :, :, at] = value.reshape(2, 2, rows, 256).astype(bf16)

    grow = [math.exp(-log_alpha * k / steps) for k in range(steps)]
    shrink = [math.exp(log_alpha * k / steps) / steps for k in range(steps)]

    def stage_sent(phase, c):
        if phase == 0:
            finish(fetches[c])
            for l in range(local_steps):
                for a in range(row_parts):
                    for half in range(2):
                        sent[c, l, a, half] = residual[l, row_at(a, half, c)].astype(bf16)
            if c == 0:
                enter()
        copies = begin(
            phase,
            c,
            0,
            everyone,
            lambda p: sent.at[c, :, p // 2, :, :, lane_at(p)],
            lambda s: timeline.at[c, pl.ds(s * local_steps, local_steps)],
        )
        if phase == 0 and c == chunks - 1:
            pass_ends()
        return copies

    def stage_spectrum(phase, c):
        @pl.loop(0, lanes // 128)
        def _(n):
            at = pl.ds(pl.multiple_of(n * 128, 128), 128)
            for half in range(2):
                values = [timeline[c, k, half, :, at].astype(f32) * grow[k] for k in range(steps)]
                spectrum = forward_fft(values)
                spec_even[c, 0, y, half, :, at] = spectrum[0][0].astype(bf16)
                spec_even[c, 0, 1 - y, half, :, at] = spectrum[steps // 2][0].astype(bf16)
                for j in range(1, steps // 2):
                    for kind in range(2):
                        value = spectrum[j][kind].astype(bf16)
                        if j % 2:
                            spec_odd[c, place_odd(j), kind, half, :, at] = value
                        else:
                            spec_even[c, place_even(j // 2), kind, half, :, at] = value

        return begin(
            phase,
            c,
            0,
            same_y,
            lambda p: spec_even.at[c, of_rank(even_rank(p))],
            lambda s: in_even.at[c, :, :, lax.rem(s // 2, 2), :, :, lane_at(s)],
        ) + begin(
            phase,
            c,
            groups,
            same_x,
            lambda p: spec_odd.at[c, of_rank(odd_rank(p))],
            lambda s: in_odd.at[c, :, :, s // 4, :, :, lane_at(s)],
        )

    def stage_wave(phase, c):
        if phase == 2 and c == 0:
            load_real.wait()
            load_imag.wait()
        for i in range(pairs):
            matmul_pair(c, i, 2 * i + 1, in_odd, wave_odd)
        copies = begin(
            phase,
            c,
            groups,
            same_x,
            lambda p: wave_odd.at[c, :, :, p // 4, :, :, lane_at(p)],
            lambda s: back_odd.at[c, of_rank(odd_rank(s))],
        )
        if phase == 2 and c == 0:
            finish_ends()
        for i in range(pairs):
            matmul_pair(c, i, 2 * i, in_even, wave_even)
        return copies + begin(
            phase,
            c,
            0,
            same_y,
            lambda p: wave_even.at[c, :, :, lax.rem(p // 2, 2), :, :, lane_at(p)],
            lambda s: back_even.at[c, of_rank(even_rank(s))],
        )

    def stage_values(phase, c):
        @pl.loop(0, lanes // 128)
        def _(n):
            at = pl.ds(pl.multiple_of(n * 128, 128), 128)
            for half in range(2):
                spectrum = [(back_even[c, 0, y, half, :, at].astype(f32), None)]
                for j in range(1, steps // 2):
                    if j % 2:
                        pair = [back_odd[c, place_odd(j), kind, half, :, at] for kind in range(2)]
                    else:
                        pair = [
                            back_even[c, place_even(j // 2), kind, half, :, at] for kind in range(2)
                        ]
                    spectrum.append(tuple(value.astype(f32) for value in pair))
                spectrum.append((back_even[c, 0, 1 - y, half, :, at].astype(f32), None))
                for k, value in enumerate(backward_fft(spectrum)):
                    val_out[c, k, half, :, at] = (value * shrink[k]).astype(bf16)

        copies = begin(
            phase,
            c,
            0,
            everyone,
            lambda p: val_out.at[c, pl.ds(p * local_steps, local_steps)],
            lambda s: corr.at[c, pl.ds(0, local_steps), s // 2, :, :, lane_at(s)],
        )
        for mask in range(1, groups):
            copy, peer = next_copy(phase // 4, c, mask)
            pl.when(takes_next(peer))(copy.start)
        pl.when(takes_next(me))(next_copy(phase // 4, c, 0)[0].start)
        return copies

    def takes_next(p):
        return (lax.rem(p, 2) == 1) & (p != groups - 1)

    def next_copy(iteration, c, d):
        peer = at_mask(d)
        row = jnp.minimum((peer + 1) * local_steps, steps - 1)
        source = val_out.at[c, row]
        target = corr.at[c, local_steps, me // 2, :, :, lane_at(me)]
        if d == 0:
            return pltpu.make_async_copy(source, target, next_own.at[iteration, c]), peer
        copy = pltpu.make_async_remote_copy(
            src_ref=source,
            dst_ref=target,
            send_sem=next_send.at[iteration, c, d],
            recv_sem=next_recv.at[iteration, c, d],
            device_id={"tm": peer},
            device_id_type=pl.DeviceIdType.MESH,
        )
        return copy, peer

    def hand_copy(iteration, c):
        return pltpu.make_async_remote_copy(
            src_ref=corr.at[c, 0],
            dst_ref=corr.at[c, local_steps],
            send_sem=hand_send.at[iteration, c],
            recv_sem=hand_recv.at[iteration, c],
            device_id={"tm": lax.rem(me + groups - 1, groups)},
            device_id_type=pl.DeviceIdType.MESH,
        )

    def await_next(iteration, c):
        for d in range(1, groups):
            copy, peer = next_copy(iteration, c, d)
            pl.when(takes_next(peer))(copy.wait_send)
            pl.when(takes_next(me))(copy.wait_recv)
        pl.when(takes_next(me))(next_copy(iteration, c, 0)[0].wait)

        @pl.when(me == groups - 1)
        def _():
            corr[c, local_steps] = jnp.zeros(corr.shape[2:], bf16)

        hand = hand_copy(iteration, c)
        pl.when(lax.rem(me, 2) == 1)(hand.wait_send)
        pl.when(lax.rem(me, 2) == 0)(hand.wait_recv)

    def update(iteration, c):
        if iteration == 0 and c == 0:
            load_jac.wait()
        pl.when(lax.rem(me, 2) == 1)(hand_copy(iteration, c).start)
        for l in range(local_steps):
            if l == local_steps - 1:
                await_next(iteration, c)
            lhs[pl.ds(0, 2 * share)] = (
                corr[c, l + 1].astype(f32).reshape(2 * share, ns).astype(bf16)
            )

            @pl.loop(0, ns // 256)
            def _(n):
                at = pl.ds(pl.multiple_of(n * 256, 256), 256)
                carried = jnp.dot(
                    lhs[pl.ds(0, 2 * share)], jac[l, :, at], preferred_element_type=f32
                )
                for a in range(row_parts):
                    for half in range(2):
                        first = (2 * a + half) * rows
                        place = row_at(a, half, c)
                        step = corr[c, l, a, half, :, at].astype(f32)
                        new = residual[l, place, at] - (step - carried[first : first + rows])
                        residual[l, place, at] = new
                        if iteration == 0:
                            adjoint[l, place, at] = step
                            sent[c, l, a, half, :, at] = new.astype(bf16)
                        else:
                            adjoint[l, place, at] += step

        outs = []
        if iteration == ITERS - 1:
            for a in range(row_parts):
                place = rows_of(a, c)
                for o, (here, there) in enumerate(
                    ((adjoint, adjoint_hbm), (residual, residual_hbm))
                ):
                    out = pltpu.make_async_copy(
                        here.at[:, place], there.at[:, place], out_sem.at[o, c, a]
                    )
                    out.start()
                    outs.append(out)
        return outs

    stages = (stage_sent, stage_spectrum, stage_wave, stage_values)
    flying = [None] * chunks
    outs = []
    for phase in range(4 * ITERS + 1):
        for c in range(chunks):
            if phase:
                finish(flying[c])
            if phase and phase % 4 == 0:
                outs += update(phase // 4 - 1, c)
            if phase < 4 * ITERS:
                flying[c] = stages[phase % 4](phase, c)
    finish(outs)


def body(objective, jacobians, precond_blocks):
    local_steps, cols, ns = objective.shape
    groups, parts = lax.axis_size("tm"), lax.axis_size("obj")
    row_parts = groups // 2
    rows = 8
    if groups != 2**3 or cols % (row_parts * 2 * rows) or local_steps % 2 or ns % (parts * 16):
        return plain_body(objective, jacobians, precond_blocks)
    chunks = cols // (row_parts * 2 * rows)
    lanes = ns // 2
    steps = groups * local_steps
    pairs = local_steps // 2
    bf16 = jnp.bfloat16
    anywhere = pl.BlockSpec(memory_space=pl.ANY)
    shape = jax.ShapeDtypeStruct(objective.shape, jnp.float32)
    by_frequency = pltpu.VMEM((chunks, steps // 4, 2, 2, rows, lanes), bf16)
    by_pair = pltpu.VMEM((chunks, pairs, 2, 2, 2, rows, ns), bf16)
    dma = pltpu.SemaphoreType.DMA
    return pl.pallas_call(
        functools.partial(kernel, groups, parts),
        out_shape=(shape, shape),
        in_specs=[anywhere, anywhere, anywhere],
        out_specs=(anywhere, anywhere),
        scratch_shapes=[
            pltpu.VMEM(objective.shape, jnp.float32),
            pltpu.VMEM(objective.shape, jnp.float32),
            pltpu.VMEM(precond_blocks.shape, bf16),
            pltpu.VMEM(jacobians.shape, bf16),
            pltpu.VMEM((chunks, local_steps, row_parts, 2, rows, ns), bf16),
            pltpu.VMEM((chunks, steps, 2, rows, lanes), bf16),
            by_frequency,
            by_frequency,
            by_pair,
            by_pair,
            by_pair,
            by_pair,
            by_frequency,
            by_frequency,
            pltpu.VMEM((chunks, steps, 2, rows, lanes), bf16),
            pltpu.VMEM((chunks, local_steps + 1, row_parts, 2, rows, ns), bf16),
            pltpu.VMEM((2 * row_parts * rows, ns), bf16),
            dma((4,)),
            dma((chunks, row_parts)),
            dma((parts,)),
            dma((parts,)),
            dma((4 * ITERS, chunks, 2)),
            dma((4 * ITERS, chunks, 2 * groups)),
            dma((4 * ITERS, chunks, 2 * groups)),
            dma((ITERS, chunks)),
            dma((ITERS, chunks, groups)),
            dma((ITERS, chunks, groups)),
            dma((ITERS, chunks)),
            dma((ITERS, chunks)),
            dma((2, chunks, row_parts)),
        ],
        compiler_params=pltpu.CompilerParams(
            collective_id=0, has_side_effects=True, vmem_limit_bytes=60 * 1024 * 1024
        ),
    )(objective, jacobians, precond_blocks)


def solution(mesh):
    in_specs = (P("tm", "obj", None), P("tm", None, None), P(None, "tm", None, None))
    out_specs = (P("tm", "obj", None), P("tm", "obj", None))
    return jax.shard_map(body, mesh=mesh, in_specs=in_specs, out_specs=out_specs, check_vma=False)
```

```python
import functools
import math

import jax
import jax.numpy as jnp
import numpy as np
from jax import lax
from jax.experimental import pallas as pl
from jax.experimental.pallas import tpu as pltpu
from jax.sharding import PartitionSpec as P

ITERS = 2
SUBS = 3

log_alpha = math.log(0.05)


def make_tables(groups, local_steps):
    steps = groups * local_steps
    mid = local_steps // 2
    per_device = 4 * mid
    forward = np.zeros((groups, per_device, steps, 2))
    backward = np.zeros((steps, 2, groups, per_device))
    k = np.arange(steps)
    grow = np.exp(k * (-log_alpha / steps))
    shrink = np.exp(k * (log_alpha / steps)) / steps

    def put(t, slot, half, frequency, kind, weight):
        angle = 2.0 * math.pi * ((frequency * k) % steps) / steps
        wave = np.cos(angle) if kind == 0 else -np.sin(angle)
        forward[t, slot, :, half] = wave * grow
        backward[:, half, t, slot] = weight * wave * shrink

    for t in range(groups):
        own = 0 if t < groups // 2 else 1
        slot = 0
        for m in range(1, mid):
            for kind in range(2):
                for half in range(2):
                    put(t, slot, half, t * local_steps + m, kind, 2.0)
                    slot += 1
        for kind in range(2):
            put(t, slot, own, t * local_steps + mid, kind, 2.0)
            slot += 1
        if (2 * t) % groups == 0:
            put(t, slot, 1 - own, t * local_steps, 0, 1.0)
            put(t, slot + 1, own, t * local_steps, 0, 1.0)
        else:
            for kind in range(2):
                put(t, slot + kind, 1 - own, t * local_steps, kind, 2.0)
    return (
        forward.reshape(groups * per_device, 2 * steps),
        backward.reshape(2 * steps, groups * per_device),
    )


def split_table(table):
    high = table.astype(jnp.bfloat16)
    low = (table - high.astype(np.float64)).astype(jnp.bfloat16)
    return jnp.asarray(high), jnp.asarray(low)


def transform(table, x):
    dims = (((1,), (0,)), ((), ()))
    high, low = table
    return lax.dot_general(high, x, dims, preferred_element_type=jnp.float32) + lax.dot_general(
        low, x, dims, preferred_element_type=jnp.float32
    )


def exchange(x):
    return lax.all_to_all(x, "tm", split_axis=0, concat_axis=0, tiled=True)


def mul(left, right):
    return jnp.dot(left, right, preferred_element_type=jnp.float32)


def complex_mul(real, imag, block_real, block_imag):
    wave_real = mul(real, block_real) - mul(imag, block_imag)
    wave_imag = mul(real, block_imag) + mul(imag, block_real)
    return wave_real.astype(jnp.bfloat16), wave_imag.astype(jnp.bfloat16)


def plain_body(objective, jacobians, precond_blocks):
    local_steps, cols, ns = objective.shape
    groups = lax.axis_size("tm")
    mid = local_steps // 2
    per_device = 4 * mid
    lane_parts = 2
    row_parts = groups // lane_parts
    rows, lanes = cols // 2 // row_parts, ns // lane_parts
    forward, backward = make_tables(groups, local_steps)
    forward, backward = split_table(forward), split_table(backward)

    def to_pieces(x):
        x = x.reshape(x.shape[0], row_parts, rows, lane_parts, lanes)
        return x.transpose(1, 3, 0, 2, 4).reshape(-1, rows, lanes)

    def from_pieces(x):
        x = x.reshape(row_parts, lane_parts, -1, rows, lanes)
        return x.transpose(2, 0, 3, 1, 4).reshape(-1, cols // 2, ns)

    adjoint = jnp.zeros_like(objective)
    residual = objective
    for iteration in range(ITERS):
        sent = residual.astype(jnp.bfloat16).reshape(2 * local_steps, cols // 2, ns)
        timeline = exchange(to_pieces(sent))
        spectrum = transform(forward, timeline).astype(jnp.bfloat16)
        spectrum = from_pieces(exchange(spectrum))
        waves = []
        slot = 0
        for m in range(1, mid):
            part = spectrum[slot : slot + 4].reshape(2, cols, ns)
            pair = complex_mul(part[0], part[1], precond_blocks[0, m], precond_blocks[1, m])
            waves += [w.reshape(2, cols // 2, ns) for w in pair]
            slot += 4
        for m in (mid, 0):
            pair = complex_mul(
                spectrum[slot], spectrum[slot + 1], precond_blocks[0, m], precond_blocks[1, m]
            )
            waves += [w[None] for w in pair]
            slot += 2
        waves = exchange(to_pieces(jnp.concatenate(waves, axis=0)))
        values = transform(backward, waves).astype(jnp.bfloat16)
        correction = from_pieces(exchange(values)).reshape(local_steps, cols, ns)
        route = [(i, i - 1) for i in range(1, groups)]
        next_row = lax.ppermute(correction[:1], "tm", route)
        following = jnp.concatenate([correction[1:], next_row], axis=0)
        carried = jnp.einsum(
            "kcn,knm->kcm", following, jacobians, preferred_element_type=jnp.float32
        )
        adjoint = adjoint + correction.astype(jnp.float32)
        residual = residual - (correction.astype(jnp.float32) - carried)
    return (adjoint, residual)


def twiddle(value, angle):
    real, imag = value
    c, s = math.cos(angle), math.sin(angle)
    if imag is None:
        return real * c, real * s
    if abs(c) < 1e-12:
        return (-imag, real) if s > 0 else (imag, -real)
    if abs(s) < 1e-12:
        return value
    return real * c - imag * s, real * s + imag * c


def forward_fft(x):
    n = len(x)
    if n == 1:
        return [(x[0], None)]
    if n == 2:
        return [(x[0] + x[1], None), (x[0] - x[1], None)]
    even, odd = forward_fft(x[0::2]), forward_fft(x[1::2])
    out = [None] * (n // 2 + 1)
    out[0] = (even[0][0] + odd[0][0], None)
    out[n // 2] = (even[0][0] - odd[0][0], None)
    for k in range(1, n // 4):
        er, ei = even[k]
        tr, ti = twiddle(odd[k], -2.0 * math.pi * k / n)
        out[k] = (er + tr, ei + ti)
        out[n // 2 - k] = (er - tr, ti - ei)
    out[n // 4] = (even[n // 4][0], -odd[n // 4][0])
    return out


def backward_fft(spectrum):
    n = 2 * (len(spectrum) - 1)
    if n == 2:
        a, b = spectrum[0][0], spectrum[1][0]
        return [a + b, a - b]
    even, odd = [], []
    for k in range(n // 4 + 1):
        if k == 0:
            a, b = spectrum[0][0], spectrum[n // 2][0]
            even.append((a + b, None))
            odd.append((a - b, None))
        elif k == n // 4:
            a, b = spectrum[k]
            even.append((a + a, None))
            odd.append((-(b + b), None))
        else:
            ar, ai = spectrum[k]
            br, bi = spectrum[n // 2 - k]
            even.append((ar + br, ai - bi))
            odd.append(twiddle((ar - br, ai + bi), 2.0 * math.pi * k / n))
    out = [None] * n
    out[0::2], out[1::2] = backward_fft(even), backward_fft(odd)
    return out


def odd_position(j, steps, x):
    local_steps = steps // 8
    for held in (j, steps - j):
        t, m = held // local_steps, held % local_steps
        if (t // 2) % 2 == x:
            return ((t // 4) * 2 + t % 2) * (local_steps // 2) + m // 2
    raise ValueError(j)


def kernel(
    groups,
    objective_hbm,
    jac_hbm,
    pre_hbm,
    adjoint_hbm,
    residual_hbm,
    adjoint,
    residual,
    weights,
    jac,
    sent,
    timeline,
    spec_even,
    spec_odd,
    in_even,
    in_odd,
    wave_even,
    wave_odd,
    back_even,
    back_odd,
    spec_far,
    in_far,
    back_far,
    val_out,
    corr,
    lhs,
    load_sem,
    objective_sem,
    own_sem,
    send_sem,
    recv_sem,
    next_own,
    next_send,
    next_recv,
    hand_send,
    hand_recv,
    out_sem,
):
    local_steps, _, ns = adjoint.shape
    steps = groups * local_steps
    pairs = local_steps // 2
    chunks, _, row_parts, subs, rows, _ = sent.shape
    lanes = timeline.shape[4]
    share = row_parts * subs * rows
    me = lax.axis_index("tm")
    y, x, core = me // 4, lax.rem(me // 2, 2), lax.rem(me, 2)
    ends = (x == 0) & (core == 0)
    sign = (1 - 2 * y).astype(jnp.float32)
    f32, bf16 = jnp.float32, jnp.bfloat16

    def at_mask(mask):
        bits = [1 - v if mask & w else v for v, w in ((y, 4), (x, 2), (core, 1))]
        return bits[0] * 4 + bits[1] * 2 + bits[2]

    def row_at(a, half, c):
        return pl.ds(((a * chunks + c) * subs + half) * rows, rows)

    def rows_of(a, c):
        return pl.ds((a * chunks + c) * subs * rows, subs * rows)

    fetches = [
        [
            pltpu.make_async_copy(
                objective_hbm.at[:, rows_of(a, c)],
                residual.at[:, rows_of(a, c)],
                objective_sem.at[c, a],
            )
            for a in range(row_parts)
        ]
        for c in range(chunks)
    ]
    for group in fetches:
        for fetch in group:
            fetch.start()

    load_real = pltpu.make_async_copy(pre_hbm.at[0], weights.at[0], load_sem.at[0])
    load_imag = pltpu.make_async_copy(pre_hbm.at[1], weights.at[1], load_sem.at[1])
    load_jac = pltpu.make_async_copy(jac_hbm, jac, load_sem.at[2])

    barrier = pltpu.get_barrier_semaphore()
    for mask in range(1, groups):
        pl.semaphore_signal(
            barrier,
            inc=1,
            device_id={"tm": at_mask(mask)},
            device_id_type=pl.DeviceIdType.MESH,
        )

    load_real.start()
    load_imag.start()
    load_jac.start()

    def lane_at(p):
        return pl.ds(pl.multiple_of(lax.rem(p, 2) * lanes, lanes), lanes)

    def begin(phase, c, slot, masks, source, target):
        copies = []
        for mask in masks:
            peer = at_mask(mask)
            copy = pltpu.make_async_remote_copy(
                src_ref=source(peer),
                dst_ref=target(me),
                send_sem=send_sem.at[phase, c, slot + mask],
                recv_sem=recv_sem.at[phase, c, slot + mask],
                device_id={"tm": peer},
                device_id_type=pl.DeviceIdType.MESH,
            )
            copy.start()
            copies.append(copy)
        own = pltpu.make_async_copy(source(me), target(me), own_sem.at[phase, c, slot // groups])
        own.start()
        return copies + [own]

    everyone = (6, 2, 4, 3, 5, 7, 1)
    same_y, same_x = (2, 3, 1), (4, 5, 1)

    def finish(copies):
        for copy in copies:
            copy.wait()

    def even_rank(p):
        return lax.rem(p, 4)

    def odd_rank(p):
        return (p // 4) * 2 + lax.rem(p, 2)

    def of_rank(rank):
        return pl.ds(rank * pairs, pairs)

    def place_even(e):
        return jnp.where(y == 0, e, (steps // 4 - e) % (steps // 4))

    def place_odd(j):
        return jnp.where(x == 0, odd_position(j, steps, 0), odd_position(j, steps, 1))

    def matmul_pair(c, i, m, source, target):
        size = 2 * subs * rows
        for kind in range(2):
            piece = source[c, i, kind].astype(f32)
            if m == 0 and kind == 1:
                piece = jnp.where(ends, in_far[c].astype(f32), piece)
            piece = piece.reshape(size, ns).astype(bf16)
            lhs[pl.ds(kind * size, size)] = piece

        for n in range(ns // 256):
            at = pl.ds(n * 256, 256)
            left = lhs[pl.ds(0, 2 * size)]
            p = jnp.dot(left, weights[0, m, :, at], preferred_element_type=f32)
            q = jnp.dot(left, weights[1, m, :, at], preferred_element_type=f32)
            real = p[:size] - sign * q[size:]
            imag = sign * q[:size] + p[size:]
            if m == 0:
                real = jnp.where(ends, p[:size], real)
                imag = jnp.where(ends, p[size:], imag)
            for kind, value in enumerate((real, imag)):
                target[c, i, kind, :, :, :, at] = value.reshape(2, subs, rows, 256).astype(bf16)

    grow = [math.exp(-log_alpha * k / steps) for k in range(steps)]
    shrink = [math.exp(log_alpha * k / steps) / steps for k in range(steps)]

    def stage_sent(phase, c):
        if phase == 0:
            if c == 0:
                pl.semaphore_wait(barrier, groups - 1)
            finish(fetches[c])
            for l in range(local_steps):
                for a in range(row_parts):
                    for half in range(subs):
                        sent[c, l, a, half] = residual[l, row_at(a, half, c)].astype(bf16)
        return begin(
            phase,
            c,
            0,
            everyone,
            lambda p: sent.at[c, :, p // 2, :, :, lane_at(p)],
            lambda s: timeline.at[c, pl.ds(s * local_steps, local_steps)],
        )

    def far_to_end(phase, c, rank):
        slot = 2 * groups + rank
        return pltpu.make_async_remote_copy(
            src_ref=spec_far.at[c],
            dst_ref=in_far.at[c, rank // 2, :, :, lane_at(rank)],
            send_sem=send_sem.at[phase, c, slot],
            recv_sem=recv_sem.at[phase, c, slot],
            device_id={"tm": (1 - y) * 4},
            device_id_type=pl.DeviceIdType.MESH,
        )

    def far_from_end(phase, c, rank):
        slot = 2 * groups + rank
        return pltpu.make_async_remote_copy(
            src_ref=wave_even.at[c, 0, 1, rank // 2, :, :, lane_at(rank)],
            dst_ref=back_far.at[c],
            send_sem=send_sem.at[phase, c, slot],
            recv_sem=recv_sem.at[phase, c, slot],
            device_id={"tm": (1 - y) * 4 + rank},
            device_id_type=pl.DeviceIdType.MESH,
        )

    def stage_spectrum(phase, c):
        @pl.loop(0, lanes // 128)
        def _(n):
            at = pl.ds(pl.multiple_of(n * 128, 128), 128)
            for half in range(subs):
                values = [timeline[c, k, half, :, at].astype(f32) * grow[k] for k in range(steps)]
                spectrum = forward_fft(values)
                first, last = spectrum[0][0], spectrum[steps // 2][0]
                spec_even[c, 0, 0, half, :, at] = jnp.where(y == 0, first, last).astype(bf16)
                spec_even[c, 0, 1, half, :, at] = jnp.zeros(first.shape, bf16)
                spec_far[c, half, :, at] = jnp.where(y == 0, last, first).astype(bf16)
                for j in range(1, steps // 2):
                    for kind in range(2):
                        value = spectrum[j][kind].astype(bf16)
                        if j % 2:
                            spec_odd[c, place_odd(j), kind, half, :, at] = value
                        else:
                            spec_even[c, place_even(j // 2), kind, half, :, at] = value

        odd = begin(
            phase,
            c,
            groups,
            same_x,
            lambda p: spec_odd.at[c, of_rank(odd_rank(p))],
            lambda s: in_odd.at[c, :, :, s // 4, :, :, lane_at(s)],
        )
        even = begin(
            phase,
            c,
            0,
            same_y,
            lambda p: spec_even.at[c, of_rank(even_rank(p))],
            lambda s: in_even.at[c, :, :, lax.rem(s // 2, 2), :, :, lane_at(s)],
        )
        far_to_end(phase, c, even_rank(me)).start()
        return odd, even

    def stage_wave(phase, c):
        if phase == 2 and c == 0:
            load_real.wait()
            load_imag.wait()
        odd, even = flying[c]
        finish(odd)
        for i in range(pairs):
            matmul_pair(c, i, 2 * i + 1, in_odd, wave_odd)
        copies = begin(
            phase,
            c,
            groups,
            same_x,
            lambda p: wave_odd.at[c, :, :, p // 4, :, :, lane_at(p)],
            lambda s: back_odd.at[c, of_rank(odd_rank(s))],
        )
        finish(even)
        far_to_end(phase - 1, c, even_rank(me)).wait_send()

        @pl.when(ends)
        def _():
            for rank in range(4):
                far_to_end(phase - 1, c, rank).wait_recv()

        for i in reversed(range(pairs)):
            matmul_pair(c, i, 2 * i, in_even, wave_even)

        @pl.when(ends)
        def _():
            for rank in range(4):
                far_from_end(phase, c, rank).start()

        return copies + begin(
            phase,
            c,
            0,
            same_y,
            lambda p: wave_even.at[c, :, :, lax.rem(p // 2, 2), :, :, lane_at(p)],
            lambda s: back_even.at[c, of_rank(even_rank(s))],
        )

    def stage_values(phase, c):
        far_from_end(phase - 1, c, even_rank(me)).wait_recv()

        @pl.when(ends)
        def _():
            for rank in range(4):
                far_from_end(phase - 1, c, rank).wait_send()

        @pl.loop(0, lanes // 128)
        def _(n):
            at = pl.ds(pl.multiple_of(n * 128, 128), 128)
            for half in range(subs):
                near = back_even[c, 0, 0, half, :, at].astype(f32)
                far = back_far[c, half, :, at].astype(f32)
                spectrum = [(jnp.where(y == 0, near, far), None)]
                for j in range(1, steps // 2):
                    if j % 2:
                        pair = [back_odd[c, place_odd(j), kind, half, :, at] for kind in range(2)]
                    else:
                        pair = [
                            back_even[c, place_even(j // 2), kind, half, :, at] for kind in range(2)
                        ]
                    spectrum.append(tuple(value.astype(f32) for value in pair))
                spectrum.append((jnp.where(y == 0, far, near), None))
                for k, value in enumerate(backward_fft(spectrum)):
                    val_out[c, k, half, :, at] = (value * shrink[k]).astype(bf16)

        copies = begin(
            phase,
            c,
            0,
            everyone,
            lambda p: val_out.at[c, pl.ds(p * local_steps, local_steps)],
            lambda s: corr.at[c, pl.ds(0, local_steps), s // 2, :, :, lane_at(s)],
        )
        for mask in range(1, groups):
            copy, peer = next_copy(phase // 4, c, mask)
            pl.when(takes_next(peer))(copy.start)
        pl.when(takes_next(me))(next_copy(phase // 4, c, 0)[0].start)
        return copies

    def takes_next(p):
        return (lax.rem(p, 2) == 1) & (p != groups - 1)

    def next_copy(iteration, c, d):
        peer = at_mask(d)
        row = jnp.minimum((peer + 1) * local_steps, steps - 1)
        source = val_out.at[c, row]
        target = corr.at[c, local_steps, me // 2, :, :, lane_at(me)]
        if d == 0:
            return pltpu.make_async_copy(source, target, next_own.at[iteration, c]), peer
        copy = pltpu.make_async_remote_copy(
            src_ref=source,
            dst_ref=target,
            send_sem=next_send.at[iteration, c, d],
            recv_sem=next_recv.at[iteration, c, d],
            device_id={"tm": peer},
            device_id_type=pl.DeviceIdType.MESH,
        )
        return copy, peer

    def hand_copy(iteration, c):
        return pltpu.make_async_remote_copy(
            src_ref=corr.at[c, 0],
            dst_ref=corr.at[c, local_steps],
            send_sem=hand_send.at[iteration, c],
            recv_sem=hand_recv.at[iteration, c],
            device_id={"tm": lax.rem(me + groups - 1, groups)},
            device_id_type=pl.DeviceIdType.MESH,
        )

    def await_next(iteration, c):
        for d in range(1, groups):
            copy, peer = next_copy(iteration, c, d)
            pl.when(takes_next(peer))(copy.wait_send)
            pl.when(takes_next(me))(copy.wait_recv)
        pl.when(takes_next(me))(next_copy(iteration, c, 0)[0].wait)

        @pl.when(me == groups - 1)
        def _():
            corr[c, local_steps] = jnp.zeros(corr.shape[2:], bf16)

        hand = hand_copy(iteration, c)
        pl.when(lax.rem(me, 2) == 1)(hand.wait_send)
        pl.when(lax.rem(me, 2) == 0)(hand.wait_recv)

    def update(iteration, c):
        if iteration == 0 and c == 0:
            load_jac.wait()
        pl.when(lax.rem(me, 2) == 1)(hand_copy(iteration, c).start)
        for l in range(local_steps):
            if l == local_steps - 1:
                await_next(iteration, c)
            lhs[pl.ds(0, share)] = corr[c, l + 1].astype(f32).reshape(share, ns).astype(bf16)

            for n in range(ns // 256):
                at = pl.ds(n * 256, 256)
                carried = jnp.dot(
                    lhs[pl.ds(0, share)], jac[l, :, at], preferred_element_type=f32
                )
                for a in range(row_parts):
                    for half in range(subs):
                        first = (subs * a + half) * rows
                        place = row_at(a, half, c)
                        step = corr[c, l, a, half, :, at].astype(f32)
                        new = residual[l, place, at] - (step - carried[first : first + rows])
                        residual[l, place, at] = new
                        if iteration == 0:
                            adjoint[l, place, at] = step
                            sent[c, l, a, half, :, at] = new.astype(bf16)
                        else:
                            adjoint[l, place, at] += step

        outs = []
        if iteration == ITERS - 1:
            for a in range(row_parts):
                place = rows_of(a, c)
                for o, (here, there) in enumerate(
                    ((adjoint, adjoint_hbm), (residual, residual_hbm))
                ):
                    out = pltpu.make_async_copy(
                        here.at[:, place], there.at[:, place], out_sem.at[o, c, a]
                    )
                    out.start()
                    outs.append(out)
        return outs

    stages = (stage_sent, stage_spectrum, stage_wave, stage_values)
    flying = [None] * chunks
    outs = []
    for phase in range(4 * ITERS + 1):
        for c in range(chunks):
            if phase and phase % 4 != 2:
                finish(flying[c])
            if phase and phase % 4 == 0:
                outs += update(phase // 4 - 1, c)
            if phase < 4 * ITERS:
                flying[c] = stages[phase % 4](phase, c)
    finish(outs)


def body(objective, jacobians, precond_blocks):
    local_steps, cols, ns = objective.shape
    groups = lax.axis_size("tm")
    row_parts = groups // 2
    rows, subs = 8, SUBS
    if groups != 2**3 or cols % (row_parts * subs * rows) or local_steps % 2:
        return plain_body(objective, jacobians, precond_blocks)
    chunks = cols // (row_parts * subs * rows)
    lanes = ns // 2
    steps = groups * local_steps
    pairs = local_steps // 2
    bf16 = jnp.bfloat16
    anywhere = pl.BlockSpec(memory_space=pl.ANY)
    shape = jax.ShapeDtypeStruct(objective.shape, jnp.float32)
    by_frequency = pltpu.VMEM((chunks, steps // 4, 2, subs, rows, lanes), bf16)
    by_pair = pltpu.VMEM((chunks, pairs, 2, 2, subs, rows, ns), bf16)
    dma = pltpu.SemaphoreType.DMA
    return pl.pallas_call(
        functools.partial(kernel, groups),
        out_shape=(shape, shape),
        in_specs=[anywhere, anywhere, anywhere],
        out_specs=(anywhere, anywhere),
        scratch_shapes=[
            pltpu.VMEM(objective.shape, jnp.float32),
            pltpu.VMEM(objective.shape, jnp.float32),
            pltpu.VMEM(precond_blocks.shape, bf16),
            pltpu.VMEM(jacobians.shape, bf16),
            pltpu.VMEM((chunks, local_steps, row_parts, subs, rows, ns), bf16),
            pltpu.VMEM((chunks, steps, subs, rows, lanes), bf16),
            by_frequency,
            by_frequency,
            by_pair,
            by_pair,
            by_pair,
            by_pair,
            by_frequency,
            by_frequency,
            pltpu.VMEM((chunks, subs, rows, lanes), bf16),
            pltpu.VMEM((chunks, 2, subs, rows, ns), bf16),
            pltpu.VMEM((chunks, subs, rows, lanes), bf16),
            pltpu.VMEM((chunks, steps, subs, rows, lanes), bf16),
            pltpu.VMEM((chunks, local_steps + 1, row_parts, subs, rows, ns), bf16),
            pltpu.VMEM((row_parts * subs * rows, ns), bf16),
            dma((3,)),
            dma((chunks, row_parts)),
            dma((4 * ITERS, chunks, 2)),
            dma((4 * ITERS, chunks, 2 * groups + 4)),
            dma((4 * ITERS, chunks, 2 * groups + 4)),
            dma((ITERS, chunks)),
            dma((ITERS, chunks, groups)),
            dma((ITERS, chunks, groups)),
            dma((ITERS, chunks)),
            dma((ITERS, chunks)),
            dma((2, chunks, row_parts)),
        ],
        compiler_params=pltpu.CompilerParams(
            collective_id=0, has_side_effects=True, vmem_limit_bytes=48 * 1024 * 1024
        ),
    )(objective, jacobians, precond_blocks)


def solution(mesh):
    in_specs = (P("tm", "obj", None), P("tm", None, None), P(None, "tm", None, None))
    out_specs = (P("tm", "obj", None), P("tm", "obj", None))
    return jax.shard_map(body, mesh=mesh, in_specs=in_specs, out_specs=out_specs, check_vma=False)
```

```python
import functools
import math

import jax
import jax.numpy as jnp
import numpy as np
from jax import lax
from jax.experimental import pallas as pl
from jax.experimental.pallas import tpu as pltpu
from jax.sharding import PartitionSpec as P

ITERS = 2
SUBS = 3

log_alpha = math.log(0.05)


def make_tables(groups, local_steps):
    steps = groups * local_steps
    mid = local_steps // 2
    per_device = 4 * mid
    forward = np.zeros((groups, per_device, steps, 2))
    backward = np.zeros((steps, 2, groups, per_device))
    k = np.arange(steps)
    grow = np.exp(k * (-log_alpha / steps))
    shrink = np.exp(k * (log_alpha / steps)) / steps

    def put(t, slot, half, frequency, kind, weight):
        angle = 2.0 * math.pi * ((frequency * k) % steps) / steps
        wave = np.cos(angle) if kind == 0 else -np.sin(angle)
        forward[t, slot, :, half] = wave * grow
        backward[:, half, t, slot] = weight * wave * shrink

    for t in range(groups):
        own = 0 if t < groups // 2 else 1
        slot = 0
        for m in range(1, mid):
            for kind in range(2):
                for half in range(2):
                    put(t, slot, half, t * local_steps + m, kind, 2.0)
                    slot += 1
        for kind in range(2):
            put(t, slot, own, t * local_steps + mid, kind, 2.0)
            slot += 1
        if (2 * t) % groups == 0:
            put(t, slot, 1 - own, t * local_steps, 0, 1.0)
            put(t, slot + 1, own, t * local_steps, 0, 1.0)
        else:
            for kind in range(2):
                put(t, slot + kind, 1 - own, t * local_steps, kind, 2.0)
    return (
        forward.reshape(groups * per_device, 2 * steps),
        backward.reshape(2 * steps, groups * per_device),
    )


def split_table(table):
    high = table.astype(jnp.bfloat16)
    low = (table - high.astype(np.float64)).astype(jnp.bfloat16)
    return jnp.asarray(high), jnp.asarray(low)


def transform(table, x):
    dims = (((1,), (0,)), ((), ()))
    high, low = table
    return lax.dot_general(high, x, dims, preferred_element_type=jnp.float32) + lax.dot_general(
        low, x, dims, preferred_element_type=jnp.float32
    )


def exchange(x):
    return lax.all_to_all(x, "tm", split_axis=0, concat_axis=0, tiled=True)


def mul(left, right):
    return jnp.dot(left, right, preferred_element_type=jnp.float32)


def complex_mul(real, imag, block_real, block_imag):
    wave_real = mul(real, block_real) - mul(imag, block_imag)
    wave_imag = mul(real, block_imag) + mul(imag, block_real)
    return wave_real.astype(jnp.bfloat16), wave_imag.astype(jnp.bfloat16)


def plain_body(objective, jacobians, precond_blocks):
    local_steps, cols, ns = objective.shape
    groups = lax.axis_size("tm")
    mid = local_steps // 2
    per_device = 4 * mid
    lane_parts = 2
    row_parts = groups // lane_parts
    rows, lanes = cols // 2 // row_parts, ns // lane_parts
    forward, backward = make_tables(groups, local_steps)
    forward, backward = split_table(forward), split_table(backward)

    def to_pieces(x):
        x = x.reshape(x.shape[0], row_parts, rows, lane_parts, lanes)
        return x.transpose(1, 3, 0, 2, 4).reshape(-1, rows, lanes)

    def from_pieces(x):
        x = x.reshape(row_parts, lane_parts, -1, rows, lanes)
        return x.transpose(2, 0, 3, 1, 4).reshape(-1, cols // 2, ns)

    adjoint = jnp.zeros_like(objective)
    residual = objective
    for iteration in range(ITERS):
        sent = residual.astype(jnp.bfloat16).reshape(2 * local_steps, cols // 2, ns)
        timeline = exchange(to_pieces(sent))
        spectrum = transform(forward, timeline).astype(jnp.bfloat16)
        spectrum = from_pieces(exchange(spectrum))
        waves = []
        slot = 0
        for m in range(1, mid):
            part = spectrum[slot : slot + 4].reshape(2, cols, ns)
            pair = complex_mul(part[0], part[1], precond_blocks[0, m], precond_blocks[1, m])
            waves += [w.reshape(2, cols // 2, ns) for w in pair]
            slot += 4
        for m in (mid, 0):
            pair = complex_mul(
                spectrum[slot], spectrum[slot + 1], precond_blocks[0, m], precond_blocks[1, m]
            )
            waves += [w[None] for w in pair]
            slot += 2
        waves = exchange(to_pieces(jnp.concatenate(waves, axis=0)))
        values = transform(backward, waves).astype(jnp.bfloat16)
        correction = from_pieces(exchange(values)).reshape(local_steps, cols, ns)
        route = [(i, i - 1) for i in range(1, groups)]
        next_row = lax.ppermute(correction[:1], "tm", route)
        following = jnp.concatenate([correction[1:], next_row], axis=0)
        carried = jnp.einsum(
            "kcn,knm->kcm", following, jacobians, preferred_element_type=jnp.float32
        )
        adjoint = adjoint + correction.astype(jnp.float32)
        residual = residual - (correction.astype(jnp.float32) - carried)
    return (adjoint, residual)


def twiddle(value, angle):
    real, imag = value
    c, s = math.cos(angle), math.sin(angle)
    if imag is None:
        return real * c, real * s
    if abs(c) < 1e-12:
        return (-imag, real) if s > 0 else (imag, -real)
    if abs(s) < 1e-12:
        return value
    return real * c - imag * s, real * s + imag * c


def forward_fft(x):
    n = len(x)
    if n == 1:
        return [(x[0], None)]
    if n == 2:
        return [(x[0] + x[1], None), (x[0] - x[1], None)]
    even, odd = forward_fft(x[0::2]), forward_fft(x[1::2])
    out = [None] * (n // 2 + 1)
    out[0] = (even[0][0] + odd[0][0], None)
    out[n // 2] = (even[0][0] - odd[0][0], None)
    for k in range(1, n // 4):
        er, ei = even[k]
        tr, ti = twiddle(odd[k], -2.0 * math.pi * k / n)
        out[k] = (er + tr, ei + ti)
        out[n // 2 - k] = (er - tr, ti - ei)
    out[n // 4] = (even[n // 4][0], -odd[n // 4][0])
    return out


def backward_fft(spectrum):
    n = 2 * (len(spectrum) - 1)
    if n == 2:
        a, b = spectrum[0][0], spectrum[1][0]
        return [a + b, a - b]
    even, odd = [], []
    for k in range(n // 4 + 1):
        if k == 0:
            a, b = spectrum[0][0], spectrum[n // 2][0]
            even.append((a + b, None))
            odd.append((a - b, None))
        elif k == n // 4:
            a, b = spectrum[k]
            even.append((a + a, None))
            odd.append((-(b + b), None))
        else:
            ar, ai = spectrum[k]
            br, bi = spectrum[n // 2 - k]
            even.append((ar + br, ai - bi))
            odd.append(twiddle((ar - br, ai + bi), 2.0 * math.pi * k / n))
    out = [None] * n
    out[0::2], out[1::2] = backward_fft(even), backward_fft(odd)
    return out


def odd_position(j, steps, x):
    local_steps = steps // 8
    for held in (j, steps - j):
        t, m = held // local_steps, held % local_steps
        if (t // 2) % 2 == x:
            return ((t // 4) * 2 + t % 2) * (local_steps // 2) + m // 2
    raise ValueError(j)


def kernel(
    groups,
    objective_hbm,
    jac_hbm,
    pre_hbm,
    adjoint_hbm,
    residual_hbm,
    adjoint,
    residual,
    weights,
    jac,
    sent,
    timeline,
    spec_even,
    spec_odd,
    in_even,
    in_odd,
    wave_even,
    wave_odd,
    back_even,
    back_odd,
    spec_far,
    in_far,
    back_far,
    val_out,
    corr,
    lhs,
    load_sem,
    objective_sem,
    own_sem,
    send_sem,
    recv_sem,
    next_own,
    next_send,
    next_recv,
    hand_send,
    hand_recv,
    out_sem,
):
    local_steps, _, ns = adjoint.shape
    steps = groups * local_steps
    pairs = local_steps // 2
    chunks, _, row_parts, subs, rows, _ = sent.shape
    lanes = timeline.shape[4]
    share = row_parts * subs * rows
    me = lax.axis_index("tm")
    y, x, core = me // 4, lax.rem(me // 2, 2), lax.rem(me, 2)
    ends = (x == 0) & (core == 0)
    sign = (1 - 2 * y).astype(jnp.float32)
    f32, bf16 = jnp.float32, jnp.bfloat16

    def at_mask(mask):
        bits = [1 - v if mask & w else v for v, w in ((y, 4), (x, 2), (core, 1))]
        return bits[0] * 4 + bits[1] * 2 + bits[2]

    def row_at(a, half, c):
        return pl.ds(((c * row_parts + a) * subs + half) * rows, rows)

    def rows_of(c):
        return pl.ds(c * share, share)

    fetches = [
        pltpu.make_async_copy(
            objective_hbm.at[:, rows_of(c)], residual.at[:, rows_of(c)], objective_sem.at[c]
        )
        for c in range(chunks)
    ]
    for fetch in fetches:
        fetch.start()

    load_real = pltpu.make_async_copy(pre_hbm.at[0], weights.at[0], load_sem.at[0])
    load_imag = pltpu.make_async_copy(pre_hbm.at[1], weights.at[1], load_sem.at[1])
    load_jac = pltpu.make_async_copy(jac_hbm, jac, load_sem.at[2])

    barrier = pltpu.get_barrier_semaphore()
    for mask in range(1, groups):
        pl.semaphore_signal(
            barrier,
            inc=1,
            device_id={"tm": at_mask(mask)},
            device_id_type=pl.DeviceIdType.MESH,
        )

    load_real.start()
    load_imag.start()
    load_jac.start()

    def lane_at(p):
        return pl.ds(pl.multiple_of(lax.rem(p, 2) * lanes, lanes), lanes)

    def begin(phase, c, slot, masks, source, target):
        copies = []
        for mask in masks:
            peer = at_mask(mask)
            copy = pltpu.make_async_remote_copy(
                src_ref=source(peer),
                dst_ref=target(me),
                send_sem=send_sem.at[phase, c, slot + mask],
                recv_sem=recv_sem.at[phase, c, slot + mask],
                device_id={"tm": peer},
                device_id_type=pl.DeviceIdType.MESH,
            )
            copy.start()
            copies.append(copy)
        own = pltpu.make_async_copy(source(me), target(me), own_sem.at[phase, c, slot // groups])
        own.start()
        return copies + [own]

    everyone = (6, 2, 4, 3, 5, 7, 1)
    same_y, same_x = (2, 3, 1), (4, 5, 1)

    def finish(copies):
        for copy in copies:
            copy.wait()

    def even_rank(p):
        return lax.rem(p, 4)

    def odd_rank(p):
        return (p // 4) * 2 + lax.rem(p, 2)

    def of_rank(rank):
        return pl.ds(rank * pairs, pairs)

    def place_even(e):
        return jnp.where(y == 0, e, (steps // 4 - e) % (steps // 4))

    def place_odd(j):
        return jnp.where(x == 0, odd_position(j, steps, 0), odd_position(j, steps, 1))

    def matmul_pair(c, i, m, source, target):
        size = 2 * subs * rows
        for kind in range(2):
            piece = source[c, i, kind].astype(f32)
            if m == 0 and kind == 1:
                piece = jnp.where(ends, in_far[c].astype(f32), piece)
            piece = piece.reshape(size, ns).astype(bf16)
            lhs[pl.ds(kind * size, size)] = piece

        for n in range(ns // 256):
            at = pl.ds(n * 256, 256)
            left = lhs[pl.ds(0, 2 * size)]
            p = jnp.dot(left, weights[0, m, :, at], preferred_element_type=f32)
            q = jnp.dot(left, weights[1, m, :, at], preferred_element_type=f32)
            real = p[:size] - sign * q[size:]
            imag = sign * q[:size] + p[size:]
            if m == 0:
                real = jnp.where(ends, p[:size], real)
                imag = jnp.where(ends, p[size:], imag)
            for kind, value in enumerate((real, imag)):
                target[c, i, kind, :, :, :, at] = value.reshape(2, subs, rows, 256).astype(bf16)

    grow = [math.exp(-log_alpha * k / steps) for k in range(steps)]
    shrink = [math.exp(log_alpha * k / steps) / steps for k in range(steps)]

    def stage_sent(phase, c):
        if phase == 0:
            fetches[c].wait()
            for l in range(local_steps):
                for a in range(row_parts):
                    for half in range(subs):
                        sent[c, l, a, half] = residual[l, row_at(a, half, c)].astype(bf16)
            if c == 0:
                pl.semaphore_wait(barrier, groups - 1)
        return begin(
            phase,
            c,
            0,
            everyone,
            lambda p: sent.at[c, :, p // 2, :, :, lane_at(p)],
            lambda s: timeline.at[c, pl.ds(s * local_steps, local_steps)],
        )

    def far_to_end(phase, c, rank):
        slot = 2 * groups + rank
        return pltpu.make_async_remote_copy(
            src_ref=spec_far.at[c],
            dst_ref=in_far.at[c, rank // 2, :, :, lane_at(rank)],
            send_sem=send_sem.at[phase, c, slot],
            recv_sem=recv_sem.at[phase, c, slot],
            device_id={"tm": (1 - y) * 4},
            device_id_type=pl.DeviceIdType.MESH,
        )

    def far_from_end(phase, c, rank):
        slot = 2 * groups + rank
        return pltpu.make_async_remote_copy(
            src_ref=wave_even.at[c, 0, 1, rank // 2, :, :, lane_at(rank)],
            dst_ref=back_far.at[c],
            send_sem=send_sem.at[phase, c, slot],
            recv_sem=recv_sem.at[phase, c, slot],
            device_id={"tm": (1 - y) * 4 + rank},
            device_id_type=pl.DeviceIdType.MESH,
        )

    def stage_spectrum(phase, c):
        @pl.loop(0, lanes // 128)
        def _(n):
            at = pl.ds(pl.multiple_of(n * 128, 128), 128)
            for half in range(subs):
                values = [timeline[c, k, half, :, at].astype(f32) * grow[k] for k in range(steps)]
                spectrum = forward_fft(values)
                first, last = spectrum[0][0], spectrum[steps // 2][0]
                spec_even[c, 0, 0, half, :, at] = jnp.where(y == 0, first, last).astype(bf16)
                spec_even[c, 0, 1, half, :, at] = jnp.zeros(first.shape, bf16)
                spec_far[c, half, :, at] = jnp.where(y == 0, last, first).astype(bf16)
                for j in range(1, steps // 2):
                    for kind in range(2):
                        value = spectrum[j][kind].astype(bf16)
                        if j % 2:
                            spec_odd[c, place_odd(j), kind, half, :, at] = value
                        else:
                            spec_even[c, place_even(j // 2), kind, half, :, at] = value

        far_to_end(phase, c, even_rank(me)).start()
        odd = begin(
            phase,
            c,
            groups,
            same_x,
            lambda p: spec_odd.at[c, of_rank(odd_rank(p))],
            lambda s: in_odd.at[c, :, :, s // 4, :, :, lane_at(s)],
        )
        even = begin(
            phase,
            c,
            0,
            same_y,
            lambda p: spec_even.at[c, of_rank(even_rank(p))],
            lambda s: in_even.at[c, :, :, lax.rem(s // 2, 2), :, :, lane_at(s)],
        )
        return odd, even

    def stage_wave(phase, c):
        if phase == 2 and c == 0:
            load_real.wait()
            load_imag.wait()
        odd, even = flying[c]
        finish(odd)
        for i in range(pairs):
            matmul_pair(c, i, 2 * i + 1, in_odd, wave_odd)
        copies = begin(
            phase,
            c,
            groups,
            same_x,
            lambda p: wave_odd.at[c, :, :, p // 4, :, :, lane_at(p)],
            lambda s: back_odd.at[c, of_rank(odd_rank(s))],
        )
        finish(even)
        far_to_end(phase - 1, c, even_rank(me)).wait_send()

        @pl.when(ends)
        def _():
            for rank in range(4):
                far_to_end(phase - 1, c, rank).wait_recv()

        for i in range(pairs):
            matmul_pair(c, i, 2 * i, in_even, wave_even)
            if i == 0:

                @pl.when(ends)
                def _():
                    for rank in range(4):
                        far_from_end(phase, c, rank).start()

        return copies + begin(
            phase,
            c,
            0,
            same_y,
            lambda p: wave_even.at[c, :, :, lax.rem(p // 2, 2), :, :, lane_at(p)],
            lambda s: back_even.at[c, of_rank(even_rank(s))],
        )

    def stage_values(phase, c):
        far_from_end(phase - 1, c, even_rank(me)).wait_recv()

        @pl.when(ends)
        def _():
            for rank in range(4):
                far_from_end(phase - 1, c, rank).wait_send()

        @pl.loop(0, lanes // 128)
        def _(n):
            at = pl.ds(pl.multiple_of(n * 128, 128), 128)
            for half in range(subs):
                near = back_even[c, 0, 0, half, :, at].astype(f32)
                far = back_far[c, half, :, at].astype(f32)
                spectrum = [(jnp.where(y == 0, near, far), None)]
                for j in range(1, steps // 2):
                    if j % 2:
                        pair = [back_odd[c, place_odd(j), kind, half, :, at] for kind in range(2)]
                    else:
                        pair = [
                            back_even[c, place_even(j // 2), kind, half, :, at] for kind in range(2)
                        ]
                    spectrum.append(tuple(value.astype(f32) for value in pair))
                spectrum.append((jnp.where(y == 0, far, near), None))
                for k, value in enumerate(backward_fft(spectrum)):
                    val_out[c, k, half, :, at] = (value * shrink[k]).astype(bf16)

        copies = begin(
            phase,
            c,
            0,
            everyone,
            lambda p: val_out.at[c, pl.ds(p * local_steps, local_steps)],
            lambda s: corr.at[c, pl.ds(0, local_steps), s // 2, :, :, lane_at(s)],
        )
        for mask in range(1, groups):
            copy, peer = next_copy(phase // 4, c, mask)
            pl.when(takes_next(peer))(copy.start)
        pl.when(takes_next(me))(next_copy(phase // 4, c, 0)[0].start)
        return copies

    def takes_next(p):
        return (lax.rem(p, 2) == 1) & (p != groups - 1)

    def next_copy(iteration, c, d):
        peer = at_mask(d)
        row = jnp.minimum((peer + 1) * local_steps, steps - 1)
        source = val_out.at[c, row]
        target = corr.at[c, local_steps, me // 2, :, :, lane_at(me)]
        if d == 0:
            return pltpu.make_async_copy(source, target, next_own.at[iteration, c]), peer
        copy = pltpu.make_async_remote_copy(
            src_ref=source,
            dst_ref=target,
            send_sem=next_send.at[iteration, c, d],
            recv_sem=next_recv.at[iteration, c, d],
            device_id={"tm": peer},
            device_id_type=pl.DeviceIdType.MESH,
        )
        return copy, peer

    def hand_copy(iteration, c):
        return pltpu.make_async_remote_copy(
            src_ref=corr.at[c, 0],
            dst_ref=corr.at[c, local_steps],
            send_sem=hand_send.at[iteration, c],
            recv_sem=hand_recv.at[iteration, c],
            device_id={"tm": lax.rem(me + groups - 1, groups)},
            device_id_type=pl.DeviceIdType.MESH,
        )

    def await_next(iteration, c):
        for d in range(1, groups):
            copy, peer = next_copy(iteration, c, d)
            pl.when(takes_next(peer))(copy.wait_send)
            pl.when(takes_next(me))(copy.wait_recv)
        pl.when(takes_next(me))(next_copy(iteration, c, 0)[0].wait)

        @pl.when(me == groups - 1)
        def _():
            corr[c, local_steps] = jnp.zeros(corr.shape[2:], bf16)

        hand = hand_copy(iteration, c)
        pl.when(lax.rem(me, 2) == 1)(hand.wait_send)
        pl.when(lax.rem(me, 2) == 0)(hand.wait_recv)

    def update(iteration, c):
        if iteration == 0 and c == 0:
            load_jac.wait()
        pl.when(lax.rem(me, 2) == 1)(hand_copy(iteration, c).start)
        for l in range(local_steps):
            if l == local_steps - 1:
                await_next(iteration, c)
            lhs[pl.ds(0, share)] = corr[c, l + 1].astype(f32).reshape(share, ns).astype(bf16)

            for n in range(ns // 256):
                at = pl.ds(n * 256, 256)
                carried = jnp.dot(
                    lhs[pl.ds(0, share)], jac[l, :, at], preferred_element_type=f32
                )
                for a in range(row_parts):
                    for half in range(subs):
                        first = (subs * a + half) * rows
                        place = row_at(a, half, c)
                        step = corr[c, l, a, half, :, at].astype(f32)
                        new = residual[l, place, at] - (step - carried[first : first + rows])
                        residual[l, place, at] = new
                        if iteration == 0:
                            adjoint[l, place, at] = step
                            sent[c, l, a, half, :, at] = new.astype(bf16)
                        else:
                            adjoint[l, place, at] += step

        outs = []
        if iteration == ITERS - 1:
            for o, (here, there) in enumerate(((adjoint, adjoint_hbm), (residual, residual_hbm))):
                out = pltpu.make_async_copy(
                    here.at[:, rows_of(c)], there.at[:, rows_of(c)], out_sem.at[o, c]
                )
                out.start()
                outs.append(out)
        return outs

    stages = (stage_sent, stage_spectrum, stage_wave, stage_values)
    flying = [None] * chunks
    outs = []
    for phase in range(4 * ITERS + 1):
        for c in range(chunks):
            if phase and phase % 4 != 2:
                finish(flying[c])
            if phase and phase % 4 == 0:
                outs += update(phase // 4 - 1, c)
            if phase < 4 * ITERS:
                flying[c] = stages[phase % 4](phase, c)
    finish(outs)


def body(objective, jacobians, precond_blocks):
    local_steps, cols, ns = objective.shape
    groups = lax.axis_size("tm")
    row_parts = groups // 2
    rows, subs = 8, SUBS
    if groups != 2**3 or cols % (row_parts * subs * rows) or local_steps % 2:
        return plain_body(objective, jacobians, precond_blocks)
    chunks = cols // (row_parts * subs * rows)
    lanes = ns // 2
    steps = groups * local_steps
    pairs = local_steps // 2
    bf16 = jnp.bfloat16
    anywhere = pl.BlockSpec(memory_space=pl.ANY)
    shape = jax.ShapeDtypeStruct(objective.shape, jnp.float32)
    by_frequency = pltpu.VMEM((chunks, steps // 4, 2, subs, rows, lanes), bf16)
    by_pair = pltpu.VMEM((chunks, pairs, 2, 2, subs, rows, ns), bf16)
    dma = pltpu.SemaphoreType.DMA
    return pl.pallas_call(
        functools.partial(kernel, groups),
        out_shape=(shape, shape),
        in_specs=[anywhere, anywhere, anywhere],
        out_specs=(anywhere, anywhere),
        scratch_shapes=[
            pltpu.VMEM(objective.shape, jnp.float32),
            pltpu.VMEM(objective.shape, jnp.float32),
            pltpu.VMEM(precond_blocks.shape, bf16),
            pltpu.VMEM(jacobians.shape, bf16),
            pltpu.VMEM((chunks, local_steps, row_parts, subs, rows, ns), bf16),
            pltpu.VMEM((chunks, steps, subs, rows, lanes), bf16),
            by_frequency,
            by_frequency,
            by_pair,
            by_pair,
            by_pair,
            by_pair,
            by_frequency,
            by_frequency,
            pltpu.VMEM((chunks, subs, rows, lanes), bf16),
            pltpu.VMEM((chunks, 2, subs, rows, ns), bf16),
            pltpu.VMEM((chunks, subs, rows, lanes), bf16),
            pltpu.VMEM((chunks, steps, subs, rows, lanes), bf16),
            pltpu.VMEM((chunks, local_steps + 1, row_parts, subs, rows, ns), bf16),
            pltpu.VMEM((row_parts * subs * rows, ns), bf16),
            dma((3,)),
            dma((chunks,)),
            dma((4 * ITERS, chunks, 2)),
            dma((4 * ITERS, chunks, 2 * groups + 4)),
            dma((4 * ITERS, chunks, 2 * groups + 4)),
            dma((ITERS, chunks)),
            dma((ITERS, chunks, groups)),
            dma((ITERS, chunks, groups)),
            dma((ITERS, chunks)),
            dma((ITERS, chunks)),
            dma((2, chunks)),
        ],
        compiler_params=pltpu.CompilerParams(
            collective_id=0, has_side_effects=True, vmem_limit_bytes=48 * 1024 * 1024
        ),
    )(objective, jacobians, precond_blocks)


def solution(mesh):
    in_specs = (P("tm", "obj", None), P("tm", None, None), P(None, "tm", None, None))
    out_specs = (P("tm", "obj", None), P("tm", "obj", None))
    return jax.shard_map(body, mesh=mesh, in_specs=in_specs, out_specs=out_specs, check_vma=False)
```
